32 devices in a mesh: gx: 16 (over z, y, x), gy: 2 (over core).
Axes of the slice: x: 2, y: 2, z: 4, core: 2. Of those that a mesh axis runs over, the one named last changes fastest.
Arguments:
- plane_xy: bfloat16 [32, 128, 128], P('gx', 'gy'), may hold values from -6 to 6
- plane_xz: bfloat16 [32, 4096], P('gx', 'gy'), may hold values from -6 to 6
- plane_yz: bfloat16 [128, 4096], P('gy', 'gx'), may hold values from -6 to 6
- w_in: bfloat16 [512, 128], replicated, may hold values from -0.5 to 0.5
- b_in: float32 [512], replicated, may hold values from -4 to 4
- w_out: bfloat16 [512, 32], replicated, may hold values from -7.071068 to 7.071068
- labels: int32 [32, 128, 32], P('gx', 'gy'), may hold values from 0 to 31
Outputs:
- grad_xy: float32 [32, 128, 128], P('gx', 'gy')
- grad_xz: float32 [32, 4096], P('gx', 'gy')
- grad_yz: float32 [128, 4096], P('gy', 'gx')
- grad_w_in: float32 [512, 128], P('gx')
- grad_b_in: float32 [512], P('gx')
- grad_w_out: float32 [512, 32], P('gx')
The draws below stay inside these ranges and needn't reach their ends.
All inputs are finite; a program needn't handle non-finite values.
Results may differ from the reference program's by a relative error of at most 0.0008.
The reference program's roundings to bfloat16 on the way (of `features`, `hidden`, `dlogits` and `dpreact`) count: a program that leaves them out, or rounds other values in their place, can miss the bound.
Values may be sent and summed in bfloat16 or wider, within the bound.
A program may use at most 64 MiB of HBM per device.

```python
import jax
import jax.numpy as jnp
from jax import lax

C = 128
HID = 512
NCLS = 32
Z = 32
X = 32
Y = 128


def draw_w_out(key, part):
    values = jnp.clip(jax.random.normal(key, (HID, NCLS), jnp.float32), -4.0, 4.0) * HID ** (-0.5)
    return values.astype(jnp.bfloat16)


def plant(array, rng, least, top_value):
    dims = array.shape
    index_at = [jax.random.randint(jax.random.fold_in(rng, axis), (), 0, dims[axis]) for axis in range(len(dims))]
    array = array.at[tuple(index_at)].set(least)
    longest = dims.index(max(dims))
    index_at[longest] = (index_at[longest] + 1) % dims[longest]
    return array.at[tuple(index_at)].set(top_value)


def steps_of(key, shape, pieces, least, largest):
    def one(axis_at, shards_of):
        heights = jax.random.uniform(jax.random.fold_in(jax.random.fold_in(key, 6), axis_at), (shards_of,), jnp.float32, least / len(pieces), largest / len(pieces))
        return jnp.repeat(jnp.exp(heights), shape[axis_at] // shards_of).reshape((-1,) + (1,) * (len(shape) - axis_at - 1))

    level = one(*pieces[0])
    for cut in pieces[1:]:
        level = level * one(*cut)
    return level


def centred(key, shape, deviation, reach, shards=(), kind=jnp.bfloat16):
    entries = deviation * jax.random.normal(key, shape, jnp.float32)
    if shards:
        entries = entries * steps_of(key, shape, shards, -0.22, 0.18)
    return jnp.clip(entries, -reach, reach).astype(kind)


def setup_inputs(seed: int = 0) -> dict:
    key_list = jax.random.split(jax.random.key(seed), 8)
    plane_xy = centred(key_list[0], (X, Y, C), 1.0, 6.0, ((0, 16), (1, 2)))
    plane_xz = centred(key_list[1], (X, Z * C), 1.0, 6.0, ((0, 16), (1, 2)))
    plane_yz = centred(key_list[2], (Y, Z * C), 1.0, 6.0, ((0, 2), (1, 16)))
    w_in = centred(key_list[3], (HID, C), C ** -0.5, 0.5)
    b_in = centred(key_list[4], (HID,), 1.0, 4.0, (), jnp.float32)
    w_out = draw_w_out(jax.random.fold_in(key_list[7], 71), 0)
    labels = plant(jax.random.randint(key_list[6], (X, Y, Z), 0, NCLS), jax.random.fold_in(key_list[6], 1), 0, NCLS - 1).astype(jnp.int32)
    return dict(plane_xy=plane_xy, plane_xz=plane_xz, plane_yz=plane_yz, w_in=w_in, b_in=b_in, w_out=w_out, labels=labels)


def block_grads(features, label_rows, w_in, b_in, w_out):
    classes = w_out.shape[1]
    preact = lax.dot_general(features, w_in, (((1,), (1,)), ((), ())), preferred_element_type=jnp.float32) + b_in
    hidden = jax.nn.softplus(preact).astype(jnp.bfloat16)
    logits = jnp.dot(hidden, w_out, preferred_element_type=jnp.float32)
    probability = jax.nn.softmax(logits, axis=-1)
    onehot = (label_rows[:, None] == jnp.arange(classes, dtype=jnp.int32)[None, :]).astype(jnp.float32)
    dlogits = (probability - onehot).astype(jnp.bfloat16)
    grad_out = lax.dot_general(hidden, dlogits, (((0,), (0,)), ((), ())), preferred_element_type=jnp.float32)
    dhidden = lax.dot_general(dlogits, w_out, (((1,), (1,)), ((), ())), preferred_element_type=jnp.float32)
    dpreact = (dhidden * jax.nn.sigmoid(preact)).astype(jnp.bfloat16)
    grad_in = lax.dot_general(dpreact, features, (((0,), (0,)), ((), ())), preferred_element_type=jnp.float32)
    grad_bias = jnp.sum(dpreact.astype(jnp.float32), axis=0)
    dfeatures = jnp.dot(dpreact, w_in, preferred_element_type=jnp.float32)
    return dfeatures, grad_in, grad_bias, grad_out


def sweep(plane_xy, xz_cube, yz_cube, labels, w_in, b_in, w_out):
    rows_y, levels, channels = yz_cube.shape

    def advance(totals, sliced):
        plane_row, xz_row, label_row = sliced
        features = (plane_row[:, None, :].astype(jnp.float32) + xz_row[None, :, :].astype(jnp.float32)
                    + yz_cube.astype(jnp.float32)).astype(jnp.bfloat16).reshape(rows_y * levels, channels)
        dfeatures, grad_in, grad_bias, grad_out = block_grads(features, label_row.reshape(rows_y * levels), w_in, b_in, w_out)
        cube = dfeatures.reshape(rows_y, levels, channels)
        total_yz, total_in, total_bias, total_out = totals
        return (total_yz + cube, total_in + grad_in, total_bias + grad_bias, total_out + grad_out), (jnp.sum(cube, axis=1), jnp.sum(cube, axis=0))

    start = (jnp.zeros((rows_y, levels, channels), jnp.float32), jnp.zeros(w_in.shape, jnp.float32),
             jnp.zeros(b_in.shape, jnp.float32), jnp.zeros(w_out.shape, jnp.float32))
    totals, outputs = lax.scan(advance, start, (plane_xy, xz_cube, labels))
    return outputs[0], outputs[1], totals[0], totals[1], totals[2], totals[3]


def reference(plane_xy, plane_xz, plane_yz, w_in, b_in, w_out, labels):
    xz_cube = plane_xz.reshape(X, Z, C)
    yz_cube = plane_yz.reshape(Y, Z, C)
    grad_xy, grad_xz, grad_yz, grad_w_in, grad_b_in, grad_w_out = sweep(plane_xy, xz_cube, yz_cube, labels, w_in, b_in, w_out)
    return grad_xy, grad_xz.reshape(X, Z * C), grad_yz.reshape(Y, Z * C), grad_w_in, grad_b_in, grad_w_out
```

```python
import functools

import jax
import jax.numpy as jnp
from jax import lax
from jax.experimental import pallas as pl
from jax.experimental.pallas import tpu as pltpu
from jax.sharding import PartitionSpec as P


def block_grads(features, label_rows, w_in, b_in, w_out):
    classes = w_out.shape[1]
    preact = (
        lax.dot_general(
            features, w_in, (((1,), (1,)), ((), ())), preferred_element_type=jnp.float32
        )
        + b_in
    )
    hidden = jax.nn.softplus(preact).astype(jnp.bfloat16)
    logits = jnp.dot(hidden, w_out, preferred_element_type=jnp.float32)
    probability = jax.nn.softmax(logits, axis=-1)
    onehot = (label_rows[:, None] == jnp.arange(classes, dtype=jnp.int32)[None, :]).astype(
        jnp.float32
    )
    dlogits = (probability - onehot).astype(jnp.bfloat16)
    grad_out = lax.dot_general(
        hidden, dlogits, (((0,), (0,)), ((), ())), preferred_element_type=jnp.float32
    )
    dhidden = lax.dot_general(
        dlogits, w_out, (((1,), (1,)), ((), ())), preferred_element_type=jnp.float32
    )
    dpreact = (dhidden * jax.nn.sigmoid(preact)).astype(jnp.bfloat16)
    grad_in = lax.dot_general(
        dpreact, features, (((0,), (0,)), ((), ())), preferred_element_type=jnp.float32
    )
    grad_bias = jnp.sum(dpreact.astype(jnp.float32), axis=0)
    dfeatures = jnp.dot(dpreact, w_in, preferred_element_type=jnp.float32)
    return (dfeatures, grad_in, grad_bias, grad_out)


def sweep(plane_xy, xz_cube, yz_cube, labels, w_in, b_in, w_out):
    rows_y, levels, channels = yz_cube.shape

    def advance(totals, sliced):
        plane_row, xz_row, label_row = sliced
        features = (
            (
                plane_row[:, None, :].astype(jnp.float32)
                + xz_row[None, :, :].astype(jnp.float32)
                + yz_cube.astype(jnp.float32)
            )
            .astype(jnp.bfloat16)
            .reshape(rows_y * levels, channels)
        )
        dfeatures, grad_in, grad_bias, grad_out = block_grads(
            features, label_row.reshape(rows_y * levels), w_in, b_in, w_out
        )
        cube = dfeatures.reshape(rows_y, levels, channels)
        total_yz, total_in, total_bias, total_out = totals
        return (
            (total_yz + cube, total_in + grad_in, total_bias + grad_bias, total_out + grad_out),
            (jnp.sum(cube, axis=1), jnp.sum(cube, axis=0)),
        )

    start = (
        jnp.zeros((rows_y, levels, channels), jnp.float32),
        jnp.zeros(w_in.shape, jnp.float32),
        jnp.zeros(b_in.shape, jnp.float32),
        jnp.zeros(w_out.shape, jnp.float32),
    )
    totals, outputs = lax.scan(advance, start, (plane_xy, xz_cube, labels))
    return (outputs[0], outputs[1], totals[0], totals[1], totals[2], totals[3])


def per_device(plane_xy, plane_xz, plane_yz, w_in, b_in, w_out, labels):
    rows_x, rows_y, channels = plane_xy.shape
    levels = labels.shape[2]
    yz_full = lax.all_gather(plane_yz, "gx", axis=1, tiled=True)
    xz_full = lax.all_gather(plane_xz, "gy", axis=1, tiled=True)
    yz_cube = yz_full.reshape(rows_y, levels, channels)
    xz_cube = xz_full.reshape(rows_x, levels, channels)
    grad_xy, part_xz, part_yz, part_in, part_bias, part_out = sweep(
        plane_xy, xz_cube, yz_cube, labels, w_in, b_in, w_out
    )
    flat_xz = part_xz.reshape(rows_x, levels * channels)
    flat_yz = part_yz.reshape(rows_y, levels * channels)
    grad_xz = lax.psum_scatter(flat_xz, "gy", scatter_dimension=1, tiled=True)
    grad_yz = lax.psum_scatter(flat_yz, "gx", scatter_dimension=1, tiled=True)
    whole_in, whole_bias, whole_out = lax.psum((part_in, part_bias, part_out), ("gx", "gy"))
    rows_hid = whole_in.shape[0] // lax.axis_size("gx")
    first_row = lax.axis_index("gx") * rows_hid
    grad_w_in = lax.dynamic_slice_in_dim(whole_in, first_row, rows_hid, 0)
    grad_b_in = lax.dynamic_slice_in_dim(whole_bias, first_row, rows_hid, 0)
    grad_w_out = lax.dynamic_slice_in_dim(whole_out, first_row, rows_hid, 0)
    return (grad_xy, grad_xz, grad_yz, grad_w_in, grad_b_in, grad_w_out)


def exchange_plan(mesh_sizes, rows_x, rows_y, levels, channels, hidden):
    chips, cores = mesh_sizes
    if levels % chips or channels % 128 or levels % cores or hidden % (chips * cores * 8):
        return None
    own_levels = levels // chips
    best = None
    for group in range(1, chips + 1):
        if chips % group or rows_y % (group * 16):
            continue
        brick_x, brick_y = rows_x * group, rows_y // group
        cost = (brick_x + brick_y) * levels
        if best is None or cost < best[0]:
            best = (cost, group, brick_x, brick_y)
    if best is None:
        return None
    _, group, brick_x, brick_y = best
    depth = None
    for tall in range(own_levels, levels // cores + 1, own_levels):
        if (levels // cores) % tall or (rows_x * tall * brick_y) % 128:
            continue
        if depth is None or brick_x * tall * brick_y <= 512:
            depth = tall
    if depth is None:
        return None
    return group, brick_x, brick_y, own_levels, depth


def head_kernel(
    plan, sizes, xy_in, xz_in, yz_in, lab_in, w_in, bias_in, w_out,
    gxy_out, gxz_out, gyz_out, gw_out,
    xy_got, xz_got, yz_got, lab_got, xy_wide, xz_wide, yz_wide, w_aug, feats,
    xy_sum, xz_send, yz_send, xy_back, xz_back, yz_back,
    gw_sum, go_sum, pack, pack_got, chip_pack, chip_got, final_got,
    s_xy, r_xy, s_lab, r_lab, s_xz, r_xz, s_yz, r_yz,
    s_bxy, r_bxy, s_bxz, r_bxz, s_byz, r_byz,
    s_pk, r_pk, s_ck, r_ck, s_fin, r_fin,
):
    chips, cores = sizes
    group, brick_x, brick_y, own_levels, depth = plan
    rows_x = xy_in.shape[0]
    channels = xy_in.shape[2]
    blocks = yz_wide.shape[0]
    half_blocks = blocks // cores
    chips_per_block = depth // own_levels
    classes = w_out.shape[1]
    hid = w_in.shape[0]
    rows = brick_x * depth * brick_y
    part = rows_x * depth * brick_y
    f32, bf16 = jnp.float32, jnp.bfloat16
    g = lax.axis_index("gx")
    c = lax.axis_index("gy")
    q = lax.rem(g, group)
    base = g - q
    me = q * cores + c

    def copy(src, dst, send, recv, chip, core):
        return pltpu.make_async_remote_copy(
            src_ref=src, dst_ref=dst, send_sem=send, recv_sem=recv,
            device_id=(chip, core), device_id_type=pl.DeviceIdType.MESH,
        )

    barrier = pltpu.get_barrier_semaphore()
    for d in range(1, chips):
        pl.semaphore_signal(barrier, inc=1, device_id=(lax.rem(g + d, chips), c), device_id_type=pl.DeviceIdType.MESH)
    for d in range(group):
        for e in range(1, cores):
            pl.semaphore_signal(
                barrier, inc=1, device_id=(base + lax.rem(q + d, group), lax.rem(c + e, cores)),
                device_id_type=pl.DeviceIdType.MESH,
            )
    pl.semaphore_wait(barrier, chips - 1 + group * (cores - 1))

    def yz_copy(src_chip, to):
        rows_of = pl.ds(pl.multiple_of(lax.rem(to, group) * brick_y, brick_y), brick_y)
        return copy(yz_in.at[rows_of], yz_got.at[src_chip], s_yz.at[to], r_yz.at[src_chip], to, c)

    def xy_copy(src, to):
        rows_of = pl.ds(pl.multiple_of(to * brick_y, brick_y), brick_y)
        return copy(xy_in.at[:, rows_of], xy_got.at[src], s_xy.at[to], r_xy.at[src], base + to, c)

    def lab_copy(src, to):
        return copy(lab_in.at[to], lab_got.at[src], s_lab.at[to], r_lab.at[src], base + to, c)

    def xz_copy(src, to):
        return copy(xz_in, xz_got.at[src], s_xz.at[to], r_xz.at[src], base + to // cores, lax.rem(to, cores))

    members = group * cores
    for d in range(chips - 1, 0, -1):
        yz_copy(g, lax.rem(g + d, chips)).start()
    for d in range(1, members):
        xz_copy(me, lax.rem(me + d, members)).start()
    for d in range(1, group):
        xy_copy(q, lax.rem(q + d, group)).start()
        lab_copy(q, lax.rem(q + d, group)).start()

    own = pl.ds(pl.multiple_of(q * brick_y, brick_y), brick_y)
    yz_got[g] = yz_in[own, :]
    xy_got[q] = xy_in[:, own, :]
    lab_got[q] = lab_in[q]
    xz_got[me] = xz_in[...]

    bias = jnp.broadcast_to(bias_in[...], (128, hid)).T
    high = bias.astype(bf16)
    rest = bias - high.astype(f32)
    middle = rest.astype(bf16)
    low = (rest - middle.astype(f32)).astype(bf16)
    lane = lax.broadcasted_iota(jnp.int32, (hid, 128), 1)
    extra = jnp.where(
        lane == 0, high.astype(f32),
        jnp.where(lane == 1, middle.astype(f32), jnp.where(lane == 2, low.astype(f32), 0.0)),
    )
    w_aug[:, :channels] = w_in[...]
    w_aug[:, channels:] = extra.astype(bf16)
    feats[:, channels:] = jnp.ones((rows, 128), bf16)
    gw_sum[...] = jnp.zeros_like(gw_sum)
    go_sum[...] = jnp.zeros_like(go_sum)
    xy_sum[...] = jnp.zeros_like(xy_sum)

    for d in range(1, group):
        xy_copy(lax.rem(q + d, group), q).wait_recv()
        lab_copy(lax.rem(q + d, group), q).wait_recv()
    for d in range(1, members):
        xz_copy(lax.rem(me + d, members), me).wait_recv()
    for d in range(1, chips):
        yz_copy(lax.rem(g + d, chips), g).wait_recv()

    xy_wide[...] = xy_got[...].astype(f32).reshape(brick_x, brick_y, channels)
    for member in range(members):
        k, e = member // cores, member % cores
        value = xz_got[member].astype(f32)
        for j in range(half_blocks):
            xz_wide[e * half_blocks + j, k * rows_x:(k + 1) * rows_x] = value[:, j * depth:(j + 1) * depth, :]
    for chip in range(chips):
        for level in range(own_levels):
            b, z = divmod(chip * own_levels + level, depth)
            yz_wide[b, z] = yz_got[chip, :, level * channels:(level + 1) * channels].astype(f32)

    contract = lambda a, b, i, j: lax.dot_general(a, b, (((i,), (j,)), ((), ())), preferred_element_type=f32)

    def byz_copy(src, to):
        return copy(yz_send.at[to], yz_back.at[src], s_byz.at[to], r_byz.at[src], to, c)

    def bxz_copy(src, to, b):
        core = b // half_blocks
        j = lax.rem(b, half_blocks)
        return copy(xz_send.at[b, to], xz_back.at[src, j], s_bxz.at[b, to], r_bxz.at[src, j], base + to, core)

    def step(i, carry):
        b = lax.rem(i + g // chips_per_block + 1, blocks)
        total = (xy_wide[...][:, None, :, :] + xz_wide[b][:, :, None, :]) + yz_wide[b][None]
        feats[:, :channels] = total.astype(bf16).reshape(rows, channels)
        x = contract(w_aug[...], feats[...], 1, 1)
        t = jnp.exp(-jnp.abs(x))
        u = 1.0 + t
        soft = jnp.maximum(x, 0.0) + (jnp.log(u) + (t - (u - 1.0)))
        hidden = soft.astype(bf16)
        slope = jnp.exp(x - soft)
        logits = contract(w_out[...], hidden, 0, 0)
        e = jnp.exp(logits - jnp.max(logits, axis=0, keepdims=True))
        probability = e / jnp.sum(e, axis=0, keepdims=True)
        lab = jnp.concatenate([lab_got[k, pl.ds(b, 1), :] for k in range(group)], axis=1)
        hit = lax.broadcasted_iota(jnp.int32, (classes, rows), 0) == lab
        dlogits = (probability - jnp.where(hit, 1.0, 0.0)).astype(bf16)
        go_sum[...] += contract(hidden, dlogits, 1, 1)
        dpre = (contract(w_out[...], dlogits, 1, 0) * slope).astype(bf16)
        gw_sum[...] += contract(dpre, feats[...], 1, 0)
        dfeat = contract(dpre, w_in[...], 0, 0).reshape(brick_x, depth, brick_y, channels)
        xy_sum[...] += jnp.sum(dfeat, axis=1)
        dyz = jnp.sum(dfeat, axis=0).reshape(chips_per_block, own_levels, brick_y, channels)
        dxz = jnp.sum(dfeat, axis=2).reshape(group, rows_x, depth, channels)
        core = b // half_blocks
        j = lax.rem(b, half_blocks)
        xz_send[b] = dxz
        for k in range(chips_per_block):
            to = b * chips_per_block + k
            yz_send[to] = dyz[k]

            @pl.when(to != g)
            def _():
                byz_copy(g, to).start()

        for k in range(group):
            @pl.when(jnp.logical_or(q != k, c != core))
            def _():
                bxz_copy(me, k, b).start()

        return carry

    lax.fori_loop(0, blocks, step, 0)

    def bxy_copy(src, to):
        rows_of = pl.ds(to * rows_x, rows_x)
        return copy(xy_sum.at[rows_of], xy_back.at[src], s_bxy.at[to], r_bxy.at[src], base + to, c)

    part_rows = hid // (chips * cores)
    pack_view = lambda a: a.reshape(chips, cores, part_rows, a.shape[-1])
    first = pack_view(gw_sum[:, :channels])
    bias_sum = gw_sum[:, channels:]
    side = jnp.where(lane == classes, bias_sum, jnp.concatenate([go_sum[...]] + [jnp.zeros((hid, 128 - classes), f32)], axis=1))
    second = pack_view(side)
    for e in range(cores):
        pack[e, :, :, :channels] = first[:, e]
        pack[e, :, :, channels:] = second[:, e]

    def pk_copy(src, to):
        return copy(pack.at[to], pack_got.at[src], s_pk.at[to], r_pk.at[src], g, to)

    for d in range(1, cores):
        pk_copy(c, lax.rem(c + d, cores)).start()
    for d in range(1, group):
        bxy_copy(q, lax.rem(q + d, group)).start()
    for d in range(1, cores):
        pk_copy(lax.rem(c + d, cores), c).wait_recv()
    mine = pack[c]
    for d in range(1, cores):
        mine = mine + pack_got[lax.rem(c + d, cores)]
    chip_pack[...] = mine

    def ck_copy(src, to):
        return copy(chip_pack.at[to], chip_got.at[src], s_ck.at[to], r_ck.at[src], to, c)

    for d in range(chips - 1, 0, -1):
        ck_copy(g, lax.rem(g + d, chips)).start()

    for d in range(1, group):
        bxy_copy(lax.rem(q + d, group), q).wait_recv()
    xy_back[q] = xy_sum[pl.ds(q * rows_x, rows_x)]
    for k in range(group):
        gxy_out[:, k * brick_y:(k + 1) * brick_y, :] = xy_back[k]
    for j in range(half_blocks):
        b = c * half_blocks + j
        for d in range(1, members):
            bxz_copy(lax.rem(me + d, members), q, b).wait_recv()
        xz_back[me, j] = xz_send[b, q]
        value = xz_back[0, j]
        for k in range(1, members):
            value = value + xz_back[k, j]
        gxz_out[:, j] = value
    for d in range(1, chips):
        byz_copy(lax.rem(g + d, chips), g).wait_recv()
    yz_back[g] = yz_send[g]
    for k in range(group):
        value = yz_back[k]
        for p in range(1, chips // group):
            value = value + yz_back[p * group + k]
        for level in range(own_levels):
            gyz_out[k * brick_y:(k + 1) * brick_y, level * channels:(level + 1) * channels] = value[level]

    for d in range(1, chips):
        ck_copy(lax.rem(g + d, chips), g).wait_recv()
    chip_got[g] = chip_pack[g]
    value = chip_got[0]
    for k in range(1, chips):
        value = value + chip_got[k]
    final_got[c] = value

    def fin_copy(src, to):
        return copy(final_got.at[src], final_got.at[src], s_fin.at[to], r_fin.at[src], g, to)

    for d in range(1, cores):
        fin_copy(c, lax.rem(c + d, cores)).start()
    for d in range(1, cores):
        fin_copy(lax.rem(c + d, cores), c).wait_recv()
    for e in range(cores):
        gw_out[e * part_rows:(e + 1) * part_rows, :] = final_got[e]

    for d in range(1, chips):
        to = lax.rem(g + d, chips)
        yz_copy(g, to).wait_send()
        byz_copy(g, to).wait_send()
        ck_copy(g, to).wait_send()
    for d in range(1, members):
        xz_copy(me, lax.rem(me + d, members)).wait_send()
    for d in range(1, group):
        to = lax.rem(q + d, group)
        xy_copy(q, to).wait_send()
        lab_copy(q, to).wait_send()
        bxy_copy(q, to).wait_send()
    for d in range(1, cores):
        to = lax.rem(c + d, cores)
        pk_copy(c, to).wait_send()
        fin_copy(c, to).wait_send()
    for b in range(blocks):
        for k in range(group):
            @pl.when(jnp.logical_or(q != k, c != b // half_blocks))
            def _():
                bxz_copy(me, k, b).wait_send()


def per_device_kernel(plan, sizes, plane_xy, plane_xz, plane_yz, w_in, b_in, w_out, labels):
    chips, cores = sizes
    group, brick_x, brick_y, own_levels, depth = plan
    rows_x, rows_y, channels = plane_xy.shape
    levels = labels.shape[2]
    hid, classes = w_out.shape
    blocks = levels // depth
    half_blocks = blocks // cores
    members = group * cores
    rows = brick_x * depth * brick_y
    part = rows_x * depth * brick_y
    part_rows = hid // (chips * cores)
    f32, bf16 = jnp.float32, jnp.bfloat16
    lab = labels.reshape(rows_x, group, brick_y, blocks, depth).transpose(1, 3, 0, 4, 2).reshape(group, blocks, part)
    xz = plane_xz.reshape(rows_x, levels // cores, channels)
    vmem = pl.BlockSpec(memory_space=pltpu.VMEM)
    dma = pltpu.SemaphoreType.DMA
    wide = channels + 128
    gxy, gxz, gyz, gw = pl.pallas_call(
        functools.partial(head_kernel, plan, sizes),
        out_shape=[
            jax.ShapeDtypeStruct((rows_x, rows_y, channels), f32),
            jax.ShapeDtypeStruct((rows_x, half_blocks, depth, channels), f32),
            jax.ShapeDtypeStruct((rows_y, own_levels * channels), f32),
            jax.ShapeDtypeStruct((part_rows * cores, wide), f32),
        ],
        in_specs=[vmem] * 7,
        out_specs=[vmem] * 4,
        scratch_shapes=[
            pltpu.VMEM((group, rows_x, brick_y, channels), bf16),
            pltpu.VMEM((members, rows_x, levels // cores, channels), bf16),
            pltpu.VMEM((chips, brick_y, own_levels * channels), bf16),
            pltpu.VMEM((group, blocks, part), jnp.int32),
            pltpu.VMEM((brick_x, brick_y, channels), f32),
            pltpu.VMEM((blocks, brick_x, depth, channels), f32),
            pltpu.VMEM((blocks, depth, brick_y, channels), f32),
            pltpu.VMEM((hid, wide), bf16),
            pltpu.VMEM((rows, wide), bf16),
            pltpu.VMEM((brick_x, brick_y, channels), f32),
            pltpu.VMEM((blocks, group, rows_x, depth, channels), f32),
            pltpu.VMEM((chips, own_levels, brick_y, channels), f32),
            pltpu.VMEM((group, rows_x, brick_y, channels), f32),
            pltpu.VMEM((members, half_blocks, rows_x, depth, channels), f32),
            pltpu.VMEM((chips, own_levels, brick_y, channels), f32),
            pltpu.VMEM((hid, wide), f32),
            pltpu.VMEM((hid, classes), f32),
            pltpu.VMEM((cores, chips, part_rows, wide), f32),
            pltpu.VMEM((cores, chips, part_rows, wide), f32),
            pltpu.VMEM((chips, part_rows, wide), f32),
            pltpu.VMEM((chips, part_rows, wide), f32),
            pltpu.VMEM((cores, part_rows, wide), f32),
            dma((group,)), dma((group,)), dma((group,)), dma((group,)),
            dma((members,)), dma((members,)), dma((chips,)), dma((chips,)),
            dma((group,)), dma((group,)),
            dma((blocks, group)), dma((members, half_blocks)),
            dma((chips,)), dma((chips,)),
            dma((cores,)), dma((cores,)), dma((chips,)), dma((chips,)),
            dma((cores,)), dma((cores,)),
        ],
        compiler_params=pltpu.CompilerParams(
            collective_id=0, has_side_effects=True, vmem_limit_bytes=60000 * 1024
        ),
        name="occupancy_head_backward",
    )(plane_xy, xz, plane_yz, lab, w_in, b_in.reshape(1, hid), w_out)
    return (
        gxy,
        gxz.reshape(plane_xz.shape),
        gyz,
        gw[:, :channels],
        gw[:, channels + classes],
        gw[:, channels:channels + classes],
    )


def solution(mesh):
    sizes = (mesh.shape["gx"], mesh.shape["gy"])

    def body(plane_xy, plane_xz, plane_yz, w_in, b_in, w_out, labels):
        rows_x, rows_y, channels = plane_xy.shape
        plan = exchange_plan(sizes, rows_x, rows_y, labels.shape[2], channels, w_in.shape[0])
        arrays = (plane_xy, plane_xz, plane_yz, w_in, b_in, w_out, labels)
        if plan is None or w_out.shape[1] >= 128:
            return per_device(*arrays)
        return per_device_kernel(plan, sizes, *arrays)

    placed = (P("gx", "gy", None), P("gx", "gy"), P("gy", "gx"), P(), P(), P(), P("gx", "gy", None))
    return jax.shard_map(
        body,
        mesh=mesh,
        in_specs=placed,
        out_specs=(
            P("gx", "gy", None),
            P("gx", "gy"),
            P("gy", "gx"),
            P("gx", None),
            P("gx"),
            P("gx", None),
        ),
        check_vma=False,
    )
```

```python
import functools

import jax
import jax.numpy as jnp
from jax import lax
from jax.experimental import pallas as pl
from jax.experimental.pallas import tpu as pltpu
from jax.sharding import PartitionSpec as P


def block_grads(features, label_rows, w_in, b_in, w_out):
    classes = w_out.shape[1]
    preact = (
        lax.dot_general(
            features, w_in, (((1,), (1,)), ((), ())), preferred_element_type=jnp.float32
        )
        + b_in
    )
    hidden = jax.nn.softplus(preact).astype(jnp.bfloat16)
    logits = jnp.dot(hidden, w_out, preferred_element_type=jnp.float32)
    probability = jax.nn.softmax(logits, axis=-1)
    onehot = (label_rows[:, None] == jnp.arange(classes, dtype=jnp.int32)[None, :]).astype(
        jnp.float32
    )
    dlogits = (probability - onehot).astype(jnp.bfloat16)
    grad_out = lax.dot_general(
        hidden, dlogits, (((0,), (0,)), ((), ())), preferred_element_type=jnp.float32
    )
    dhidden = lax.dot_general(
        dlogits, w_out, (((1,), (1,)), ((), ())), preferred_element_type=jnp.float32
    )
    dpreact = (dhidden * jax.nn.sigmoid(preact)).astype(jnp.bfloat16)
    grad_in = lax.dot_general(
        dpreact, features, (((0,), (0,)), ((), ())), preferred_element_type=jnp.float32
    )
    grad_bias = jnp.sum(dpreact.astype(jnp.float32), axis=0)
    dfeatures = jnp.dot(dpreact, w_in, preferred_element_type=jnp.float32)
    return (dfeatures, grad_in, grad_bias, grad_out)


def sweep(plane_xy, xz_cube, yz_cube, labels, w_in, b_in, w_out):
    rows_y, levels, channels = yz_cube.shape

    def advance(totals, sliced):
        plane_row, xz_row, label_row = sliced
        features = (
            (
                plane_row[:, None, :].astype(jnp.float32)
                + xz_row[None, :, :].astype(jnp.float32)
                + yz_cube.astype(jnp.float32)
            )
            .astype(jnp.bfloat16)
            .reshape(rows_y * levels, channels)
        )
        dfeatures, grad_in, grad_bias, grad_out = block_grads(
            features, label_row.reshape(rows_y * levels), w_in, b_in, w_out
        )
        cube = dfeatures.reshape(rows_y, levels, channels)
        total_yz, total_in, total_bias, total_out = totals
        return (
            (total_yz + cube, total_in + grad_in, total_bias + grad_bias, total_out + grad_out),
            (jnp.sum(cube, axis=1), jnp.sum(cube, axis=0)),
        )

    start = (
        jnp.zeros((rows_y, levels, channels), jnp.float32),
        jnp.zeros(w_in.shape, jnp.float32),
        jnp.zeros(b_in.shape, jnp.float32),
        jnp.zeros(w_out.shape, jnp.float32),
    )
    totals, outputs = lax.scan(advance, start, (plane_xy, xz_cube, labels))
    return (outputs[0], outputs[1], totals[0], totals[1], totals[2], totals[3])


def per_device(plane_xy, plane_xz, plane_yz, w_in, b_in, w_out, labels):
    rows_x, rows_y, channels = plane_xy.shape
    levels = labels.shape[2]
    yz_full = lax.all_gather(plane_yz, "gx", axis=1, tiled=True)
    xz_full = lax.all_gather(plane_xz, "gy", axis=1, tiled=True)
    yz_cube = yz_full.reshape(rows_y, levels, channels)
    xz_cube = xz_full.reshape(rows_x, levels, channels)
    grad_xy, part_xz, part_yz, part_in, part_bias, part_out = sweep(
        plane_xy, xz_cube, yz_cube, labels, w_in, b_in, w_out
    )
    flat_xz = part_xz.reshape(rows_x, levels * channels)
    flat_yz = part_yz.reshape(rows_y, levels * channels)
    grad_xz = lax.psum_scatter(flat_xz, "gy", scatter_dimension=1, tiled=True)
    grad_yz = lax.psum_scatter(flat_yz, "gx", scatter_dimension=1, tiled=True)
    whole_in, whole_bias, whole_out = lax.psum((part_in, part_bias, part_out), ("gx", "gy"))
    rows_hid = whole_in.shape[0] // lax.axis_size("gx")
    first_row = lax.axis_index("gx") * rows_hid
    grad_w_in = lax.dynamic_slice_in_dim(whole_in, first_row, rows_hid, 0)
    grad_b_in = lax.dynamic_slice_in_dim(whole_bias, first_row, rows_hid, 0)
    grad_w_out = lax.dynamic_slice_in_dim(whole_out, first_row, rows_hid, 0)
    return (grad_xy, grad_xz, grad_yz, grad_w_in, grad_b_in, grad_w_out)


def exchange_plan(mesh_sizes, rows_x, rows_y, levels, channels, hidden):
    chips, cores = mesh_sizes
    if levels % chips or channels % 128 or levels % cores or hidden % (chips * cores * 8):
        return None
    own_levels = levels // chips
    best = None
    for group in range(1, chips + 1):
        if chips % group or rows_y % (group * 16):
            continue
        brick_x, brick_y = rows_x * group, rows_y // group
        cost = (brick_x + brick_y) * levels
        if best is None or cost < best[0]:
            best = (cost, group, brick_x, brick_y)
    if best is None:
        return None
    _, group, brick_x, brick_y = best
    depth = None
    for tall in range(own_levels, levels // cores + 1, own_levels):
        if (levels // cores) % tall or (rows_x * tall * brick_y) % 128:
            continue
        if depth is None or brick_x * tall * brick_y <= 512:
            depth = tall
    if depth is None or depth & (depth - 1) or brick_y & (brick_y - 1):
        return None
    return group, brick_x, brick_y, own_levels, depth


def head_kernel(
    plan, sizes, xy_in, xz_in, yz_in, lab_in, w_in, bias_in, w_out,
    gxy_out, gxz_out, gyz_out, gw_out, gb_out, go_out,
    xy_got, xz_got, yz_got, lab_got, xy_wide, xz_wide, lab_rows, w_aug, feats,
    xy_sum, xz_send, yz_send, xy_back, xz_back, yz_back,
    gw_sum, go_sum, pack, pack_got, chip_pack, chip_got, final_got,
    s_xy, r_xy, s_lab, r_lab, s_xz, r_xz, s_yz, r_yz,
    s_bxy, r_bxy, s_bxz, r_bxz, s_byz, r_byz,
    s_pk, r_pk, s_ck, r_ck, s_fin, r_fin,
):
    chips, cores = sizes
    group, brick_x, brick_y, own_levels, depth = plan
    rows_x = xy_in.shape[0]
    channels = xy_in.shape[2]
    blocks = xz_wide.shape[0]
    half_blocks = blocks // cores
    chips_per_block = depth // own_levels
    classes, hid = w_out.shape
    levels = blocks * depth
    rows = brick_x * depth * brick_y
    f32, bf16 = jnp.float32, jnp.bfloat16
    g = lax.axis_index("gx")
    c = lax.axis_index("gy")
    q = lax.rem(g, group)
    base = g - q
    me = q * cores + c

    def copy(src, dst, send, recv, chip, core):
        return pltpu.make_async_remote_copy(
            src_ref=src, dst_ref=dst, send_sem=send, recv_sem=recv,
            device_id=(chip, core), device_id_type=pl.DeviceIdType.MESH,
        )

    barrier = pltpu.get_barrier_semaphore()
    for d in range(1, chips):
        pl.semaphore_signal(barrier, inc=1, device_id=(lax.rem(g + d, chips), c), device_id_type=pl.DeviceIdType.MESH)
    for d in range(group):
        for e in range(1, cores):
            pl.semaphore_signal(
                barrier, inc=1, device_id=(base + lax.rem(q + d, group), lax.rem(c + e, cores)),
                device_id_type=pl.DeviceIdType.MESH,
            )

    def yz_copy(src_chip, to):
        rows_of = pl.ds(pl.multiple_of(lax.rem(to, group) * brick_y, brick_y), brick_y)
        return copy(yz_in.at[rows_of], yz_got.at[src_chip], s_yz.at[to], r_yz.at[src_chip], to, c)

    def xy_copy(src, to):
        rows_of = pl.ds(pl.multiple_of(to * brick_y, brick_y), brick_y)
        return copy(xy_in.at[:, rows_of], xy_got.at[src], s_xy.at[to], r_xy.at[src], base + to, c)

    def lab_copy(src, to):
        return copy(lab_in, lab_got.at[src], s_lab.at[to], r_lab.at[src], base + to, c)

    def xz_copy(src, to):
        return copy(xz_in, xz_got.at[src], s_xz.at[to], r_xz.at[src], base + to // cores, lax.rem(to, cores))

    members = group * cores
    own = pl.ds(pl.multiple_of(q * brick_y, brick_y), brick_y)
    yz_got[g] = yz_in[own, :]
    xy_got[q] = xy_in[:, own, :]
    lab_got[q] = lab_in[...]
    xz_got[me] = xz_in[...]

    bias = jnp.broadcast_to(bias_in[...], (128, hid)).T
    high = bias.astype(bf16)
    rest = bias - high.astype(f32)
    middle = rest.astype(bf16)
    low = (rest - middle.astype(f32)).astype(bf16)
    lane = lax.broadcasted_iota(jnp.int32, (hid, 128), 1)
    extra = jnp.where(
        lane == 0, high.astype(f32),
        jnp.where(lane == 1, middle.astype(f32), jnp.where(lane == 2, low.astype(f32), 0.0)),
    )
    w_aug[:, :channels] = w_in[...]
    w_aug[:, channels:] = extra.astype(bf16)
    feats[:, channels:] = jnp.ones((rows, 128), bf16)
    gw_sum[...] = jnp.zeros_like(gw_sum)
    go_sum[...] = jnp.zeros_like(go_sum)
    xy_sum[...] = jnp.zeros_like(xy_sum)

    pl.semaphore_wait(barrier, chips - 1 + group * (cores - 1))
    for d in range(1, group):
        xy_copy(q, lax.rem(q + d, group)).start()
        lab_copy(q, lax.rem(q + d, group)).start()
    for d in range(1, members):
        xz_copy(me, lax.rem(me + d, members)).start()
    for d in range(chips - 1, 0, -1):
        yz_copy(g, lax.rem(g + d, chips)).start()

    contract = lambda a, b, i, j: lax.dot_general(a, b, (((i,), (j,)), ((), ())), preferred_element_type=f32)

    y_bits, z_bits = brick_y.bit_length() - 1, depth.bit_length() - 1
    all_y = lab_in.shape[2]
    column = lax.broadcasted_iota(jnp.int32, (all_y, rows), 1)
    x_of = lax.shift_right_logical(column, y_bits + z_bits)
    same_y = lax.broadcasted_iota(jnp.int32, (all_y, rows), 0) == (column & (brick_y - 1)) + q * brick_y

    for d in range(1, group):
        xy_copy(lax.rem(q + d, group), q).wait_recv()
        lab_copy(lax.rem(q + d, group), q).wait_recv()
    xy_wide[...] = xy_got[...].astype(f32).reshape(brick_x, brick_y, channels)
    found = jnp.zeros((levels, rows), f32)
    for x in range(brick_x):
        spread = jnp.where(same_y & (x_of == x), 1.0, 0.0).astype(bf16)
        found += contract(lab_got[x // rows_x, x % rows_x].astype(f32).astype(bf16), spread, 1, 0)
    lab_rows[...] = found
    for d in range(1, members):
        xz_copy(lax.rem(me + d, members), me).wait_recv()
    for member in range(members):
        k, e = member // cores, member % cores
        for z in range(levels // cores):
            b, level = divmod(e * (levels // cores) + z, depth)
            xz_wide[b, k * rows_x:(k + 1) * rows_x, level, :] = xz_got[member, :, z * channels:(z + 1) * channels].astype(f32)


    def byz_copy(src, to):
        return copy(yz_send.at[to], yz_back.at[src], s_byz.at[to], r_byz.at[src], to, c)

    def bxz_copy(src, to, b):
        core = b // half_blocks
        j = lax.rem(b, half_blocks)
        return copy(xz_send.at[b, to], xz_back.at[src, j], s_bxz.at[b, to], r_bxz.at[src, j], base + to, core)

    def step(i, carry):
        b = lax.rem(i + g // chips_per_block, blocks)
        for k in range(chips_per_block):
            chip = b * chips_per_block + k

            @pl.when(chip != g)
            def _():
                yz_copy(chip, g).wait_recv()

        yz_block = jnp.stack([
            yz_got[b * chips_per_block + k, :, level * channels:(level + 1) * channels].astype(f32)
            for k in range(chips_per_block) for level in range(own_levels)
        ])
        total = (xy_wide[...][:, None, :, :] + xz_wide[b][:, :, None, :]) + yz_block[None]
        feats[:, :channels] = total.astype(bf16).reshape(rows, channels)
        x = contract(w_aug[...], feats[...], 1, 1)
        t = jnp.exp(-jnp.abs(x))
        u = 1.0 + t
        soft = jnp.maximum(x, 0.0) + (jnp.log(u) + (t - (u - 1.0)))
        hidden = soft.astype(bf16)
        slope = jnp.exp(x - soft)
        logits = contract(w_out[...], hidden, 1, 0)
        e = jnp.exp(logits - jnp.max(logits, axis=0, keepdims=True))
        probability = e / jnp.sum(e, axis=0, keepdims=True)
        at = lax.broadcasted_iota(jnp.int32, (levels, rows), 1)
        level_of = b * depth + (lax.shift_right_logical(at, y_bits) & (depth - 1))
        mine = lax.broadcasted_iota(jnp.int32, (levels, rows), 0) == level_of
        lab = jnp.sum(jnp.where(mine, lab_rows[...], 0.0), axis=0, keepdims=True)
        hit = lax.broadcasted_iota(jnp.int32, (classes, rows), 0).astype(f32) == lab
        dlogits = (probability - jnp.where(hit, 1.0, 0.0)).astype(bf16)
        go_sum[...] += contract(hidden, dlogits, 1, 1)
        dpre = (contract(w_out[...], dlogits, 0, 0) * slope).astype(bf16)
        gw_sum[...] += contract(dpre, feats[...], 1, 0)
        dfeat = contract(dpre, w_in[...], 0, 0).reshape(brick_x, depth, brick_y, channels)
        xy_sum[...] += jnp.sum(dfeat, axis=1)
        dyz = jnp.sum(dfeat, axis=0).reshape(chips_per_block, own_levels, brick_y, channels)
        dxz = jnp.sum(dfeat, axis=2).reshape(group, rows_x, depth, channels)
        core = b // half_blocks
        j = lax.rem(b, half_blocks)
        xz_send[b] = dxz
        for k in range(chips_per_block):
            to = b * chips_per_block + k
            yz_send[to] = dyz[k]

            @pl.when(to != g)
            def _():
                byz_copy(g, to).start()

        for k in range(group):
            @pl.when(jnp.logical_or(q != k, c != core))
            def _():
                bxz_copy(me, k, b).start()

        return carry

    lax.fori_loop(0, blocks, step, 0)

    def bxy_copy(src, to):
        rows_of = pl.ds(to * rows_x, rows_x)
        return copy(xy_sum.at[rows_of], xy_back.at[src], s_bxy.at[to], r_bxy.at[src], base + to, c)

    part_rows = hid // (chips * cores)
    pack_view = lambda a: a.reshape(chips, cores, part_rows, a.shape[-1])
    first = pack_view(gw_sum[:, :channels])
    bias_sum = gw_sum[:, channels:]
    side = jnp.where(lane == classes, bias_sum, jnp.concatenate([go_sum[...]] + [jnp.zeros((hid, 128 - classes), f32)], axis=1))
    second = pack_view(side)
    for e in range(cores):
        pack[e, :, :, :channels] = first[:, e]
        pack[e, :, :, channels:] = second[:, e]

    def pk_copy(src, to):
        return copy(pack.at[to], pack_got.at[src], s_pk.at[to], r_pk.at[src], g, to)

    for d in range(1, cores):
        pk_copy(c, lax.rem(c + d, cores)).start()
    for d in range(1, group):
        bxy_copy(q, lax.rem(q + d, group)).start()
    for d in range(1, cores):
        pk_copy(lax.rem(c + d, cores), c).wait_recv()
    mine = pack[c]
    for d in range(1, cores):
        mine = mine + pack_got[lax.rem(c + d, cores)]
    chip_pack[...] = mine

    def ck_copy(src, to):
        return copy(chip_pack.at[to], chip_got.at[src], s_ck.at[to], r_ck.at[src], to, c)

    for d in range(chips - 1, 0, -1):
        ck_copy(g, lax.rem(g + d, chips)).start()

    for d in range(1, group):
        bxy_copy(lax.rem(q + d, group), q).wait_recv()
    xy_back[q] = xy_sum[pl.ds(q * rows_x, rows_x)]
    for k in range(group):
        gxy_out[:, k * brick_y:(k + 1) * brick_y, :] = xy_back[k]
    for j in range(half_blocks):
        b = c * half_blocks + j
        for d in range(1, members):
            bxz_copy(lax.rem(me + d, members), q, b).wait_recv()
        xz_back[me, j] = xz_send[b, q]
        value = xz_back[0, j]
        for k in range(1, members):
            value = value + xz_back[k, j]
        for z in range(depth):
            at = (j * depth + z) * channels
            gxz_out[:, at:at + channels] = value[:, z, :]
    for d in range(1, chips):
        byz_copy(lax.rem(g + d, chips), g).wait_recv()
    yz_back[g] = yz_send[g]
    for k in range(group):
        value = yz_back[k]
        for p in range(1, chips // group):
            value = value + yz_back[p * group + k]
        for level in range(own_levels):
            gyz_out[k * brick_y:(k + 1) * brick_y, level * channels:(level + 1) * channels] = value[level]

    for d in range(1, chips):
        ck_copy(lax.rem(g + d, chips), g).wait_recv()
    chip_got[g] = chip_pack[g]
    value = chip_got[0]
    for k in range(1, chips):
        value = value + chip_got[k]
    final_got[c] = value

    def fin_copy(src, to):
        return copy(final_got.at[src], final_got.at[src], s_fin.at[to], r_fin.at[src], g, to)

    for d in range(1, cores):
        fin_copy(c, lax.rem(c + d, cores)).start()
    for d in range(1, cores):
        fin_copy(lax.rem(c + d, cores), c).wait_recv()
    for e in range(cores):
        gw_out[e * part_rows:(e + 1) * part_rows, :] = final_got[e, :, :channels]
    side = final_got[...].reshape(cores * part_rows, channels + 128)[:, channels:]
    go_out[...] = side[:, :classes]
    gb_out[...] = side.T[classes:classes + 1, :]

    for d in range(1, chips):
        to = lax.rem(g + d, chips)
        yz_copy(g, to).wait_send()
        byz_copy(g, to).wait_send()
        ck_copy(g, to).wait_send()
    for d in range(1, members):
        xz_copy(me, lax.rem(me + d, members)).wait_send()
    for d in range(1, group):
        to = lax.rem(q + d, group)
        xy_copy(q, to).wait_send()
        lab_copy(q, to).wait_send()
        bxy_copy(q, to).wait_send()
    for d in range(1, cores):
        to = lax.rem(c + d, cores)
        pk_copy(c, to).wait_send()
        fin_copy(c, to).wait_send()
    for b in range(blocks):
        for k in range(group):
            @pl.when(jnp.logical_or(q != k, c != b // half_blocks))
            def _():
                bxz_copy(me, k, b).wait_send()


def write_kernel(*refs):
    half = len(refs) // 2
    for src, dst in zip(refs[:half], refs[half:]):
        dst[...] = src[...]


def per_device_kernel(plan, sizes, plane_xy, plane_xz, plane_yz, w_in, b_in, w_out, labels):
    chips, cores = sizes
    group, brick_x, brick_y, own_levels, depth = plan
    rows_x, rows_y, channels = plane_xy.shape
    levels = labels.shape[2]
    hid, classes = w_out.shape
    blocks = levels // depth
    half_blocks = blocks // cores
    members = group * cores
    rows = brick_x * depth * brick_y
    part_rows = hid // (chips * cores)
    f32, bf16 = jnp.float32, jnp.bfloat16
    vmem = pl.BlockSpec(memory_space=pltpu.VMEM)
    dma = pltpu.SemaphoreType.DMA
    wide = channels + 128
    results = pl.pallas_call(
        functools.partial(head_kernel, plan, sizes),
        out_shape=[
            jax.ShapeDtypeStruct((rows_x, rows_y, channels), f32),
            jax.ShapeDtypeStruct(plane_xz.shape, f32),
            jax.ShapeDtypeStruct((rows_y, own_levels * channels), f32),
            jax.ShapeDtypeStruct((part_rows * cores, channels), f32),
            jax.ShapeDtypeStruct((1, part_rows * cores), f32),
            jax.ShapeDtypeStruct((part_rows * cores, classes), f32),
        ],
        in_specs=[vmem] * 7,
        out_specs=[vmem] * 6,
        scratch_shapes=[
            pltpu.VMEM((group, rows_x, brick_y, channels), bf16),
            pltpu.VMEM((members,) + plane_xz.shape, bf16),
            pltpu.VMEM((chips, brick_y, own_levels * channels), bf16),
            pltpu.VMEM((group, rows_x, levels, rows_y), jnp.int32),
            pltpu.VMEM((brick_x, brick_y, channels), f32),
            pltpu.VMEM((blocks, brick_x, depth, channels), f32),
            pltpu.VMEM((levels, rows), f32),
            pltpu.VMEM((hid, wide), bf16),
            pltpu.VMEM((rows, wide), bf16),
            pltpu.VMEM((brick_x, brick_y, channels), f32),
            pltpu.VMEM((blocks, group, rows_x, depth, channels), f32),
            pltpu.VMEM((chips, own_levels, brick_y, channels), f32),
            pltpu.VMEM((group, rows_x, brick_y, channels), f32),
            pltpu.VMEM((members, half_blocks, rows_x, depth, channels), f32),
            pltpu.VMEM((chips, own_levels, brick_y, channels), f32),
            pltpu.VMEM((hid, wide), f32),
            pltpu.VMEM((hid, classes), f32),
            pltpu.VMEM((cores, chips, part_rows, wide), f32),
            pltpu.VMEM((cores, chips, part_rows, wide), f32),
            pltpu.VMEM((chips, part_rows, wide), f32),
            pltpu.VMEM((chips, part_rows, wide), f32),
            pltpu.VMEM((cores, part_rows, wide), f32),
            dma((group,)), dma((group,)), dma((group,)), dma((group,)),
            dma((members,)), dma((members,)), dma((chips,)), dma((chips,)),
            dma((group,)), dma((group,)),
            dma((blocks, group)), dma((members, half_blocks)),
            dma((chips,)), dma((chips,)),
            dma((cores,)), dma((cores,)), dma((chips,)), dma((chips,)),
            dma((cores,)), dma((cores,)),
        ],
        compiler_params=pltpu.CompilerParams(
            collective_id=0, has_side_effects=True, vmem_limit_bytes=60000 * 1024
        ),
        name="occupancy_head_backward",
    )(plane_xy, plane_xz, plane_yz, labels.transpose(0, 2, 1), w_in, b_in.reshape(1, hid), w_out.T)
    gxy, gxz, gyz, gw, gb, go = pl.pallas_call(
        write_kernel,
        out_shape=[jax.ShapeDtypeStruct(a.shape, a.dtype) for a in results],
        in_specs=[vmem] * 6,
        out_specs=[vmem] * 6,
        name="write_outputs",
    )(*results)
    return gxy, gxz, gyz, gw, gb.reshape(part_rows * cores), go


def solution(mesh):
    sizes = (mesh.shape["gx"], mesh.shape["gy"])

    def body(plane_xy, plane_xz, plane_yz, w_in, b_in, w_out, labels):
        rows_x, rows_y, channels = plane_xy.shape
        plan = exchange_plan(sizes, rows_x, rows_y, labels.shape[2], channels, w_in.shape[0])
        arrays = (plane_xy, plane_xz, plane_yz, w_in, b_in, w_out, labels)
        if plan is None or w_out.shape[1] >= 128:
            return per_device(*arrays)
        return per_device_kernel(plan, sizes, *arrays)

    placed = (P("gx", "gy", None), P("gx", "gy"), P("gy", "gx"), P(), P(), P(), P("gx", "gy", None))
    return jax.shard_map(
        body,
        mesh=mesh,
        in_specs=placed,
        out_specs=(
            P("gx", "gy", None),
            P("gx", "gy"),
            P("gy", "gx"),
            P("gx", None),
            P("gx"),
            P("gx", None),
        ),
        check_vma=False,
    )
```

```python
import functools

import jax
import jax.numpy as jnp
from jax import lax
from jax.experimental import pallas as pl
from jax.experimental.pallas import tpu as pltpu
from jax.sharding import PartitionSpec as P


def block_grads(features, label_rows, w_in, b_in, w_out):
    classes = w_out.shape[1]
    preact = (
        lax.dot_general(
            features, w_in, (((1,), (1,)), ((), ())), preferred_element_type=jnp.float32
        )
        + b_in
    )
    hidden = jax.nn.softplus(preact).astype(jnp.bfloat16)
    logits = jnp.dot(hidden, w_out, preferred_element_type=jnp.float32)
    probability = jax.nn.softmax(logits, axis=-1)
    onehot = (label_rows[:, None] == jnp.arange(classes, dtype=jnp.int32)[None, :]).astype(
        jnp.float32
    )
    dlogits = (probability - onehot).astype(jnp.bfloat16)
    grad_out = lax.dot_general(
        hidden, dlogits, (((0,), (0,)), ((), ())), preferred_element_type=jnp.float32
    )
    dhidden = lax.dot_general(
        dlogits, w_out, (((1,), (1,)), ((), ())), preferred_element_type=jnp.float32
    )
    dpreact = (dhidden * jax.nn.sigmoid(preact)).astype(jnp.bfloat16)
    grad_in = lax.dot_general(
        dpreact, features, (((0,), (0,)), ((), ())), preferred_element_type=jnp.float32
    )
    grad_bias = jnp.sum(dpreact.astype(jnp.float32), axis=0)
    dfeatures = jnp.dot(dpreact, w_in, preferred_element_type=jnp.float32)
    return (dfeatures, grad_in, grad_bias, grad_out)


def sweep(plane_xy, xz_cube, yz_cube, labels, w_in, b_in, w_out):
    rows_y, levels, channels = yz_cube.shape

    def advance(totals, sliced):
        plane_row, xz_row, label_row = sliced
        features = (
            (
                plane_row[:, None, :].astype(jnp.float32)
                + xz_row[None, :, :].astype(jnp.float32)
                + yz_cube.astype(jnp.float32)
            )
            .astype(jnp.bfloat16)
            .reshape(rows_y * levels, channels)
        )
        dfeatures, grad_in, grad_bias, grad_out = block_grads(
            features, label_row.reshape(rows_y * levels), w_in, b_in, w_out
        )
        cube = dfeatures.reshape(rows_y, levels, channels)
        total_yz, total_in, total_bias, total_out = totals
        return (
            (total_yz + cube, total_in + grad_in, total_bias + grad_bias, total_out + grad_out),
            (jnp.sum(cube, axis=1), jnp.sum(cube, axis=0)),
        )

    start = (
        jnp.zeros((rows_y, levels, channels), jnp.float32),
        jnp.zeros(w_in.shape, jnp.float32),
        jnp.zeros(b_in.shape, jnp.float32),
        jnp.zeros(w_out.shape, jnp.float32),
    )
    totals, outputs = lax.scan(advance, start, (plane_xy, xz_cube, labels))
    return (outputs[0], outputs[1], totals[0], totals[1], totals[2], totals[3])


def per_device(plane_xy, plane_xz, plane_yz, w_in, b_in, w_out, labels):
    rows_x, rows_y, channels = plane_xy.shape
    levels = labels.shape[2]
    yz_full = lax.all_gather(plane_yz, "gx", axis=1, tiled=True)
    xz_full = lax.all_gather(plane_xz, "gy", axis=1, tiled=True)
    yz_cube = yz_full.reshape(rows_y, levels, channels)
    xz_cube = xz_full.reshape(rows_x, levels, channels)
    grad_xy, part_xz, part_yz, part_in, part_bias, part_out = sweep(
        plane_xy, xz_cube, yz_cube, labels, w_in, b_in, w_out
    )
    flat_xz = part_xz.reshape(rows_x, levels * channels)
    flat_yz = part_yz.reshape(rows_y, levels * channels)
    grad_xz = lax.psum_scatter(flat_xz, "gy", scatter_dimension=1, tiled=True)
    grad_yz = lax.psum_scatter(flat_yz, "gx", scatter_dimension=1, tiled=True)
    whole_in, whole_bias, whole_out = lax.psum((part_in, part_bias, part_out), ("gx", "gy"))
    rows_hid = whole_in.shape[0] // lax.axis_size("gx")
    first_row = lax.axis_index("gx") * rows_hid
    grad_w_in = lax.dynamic_slice_in_dim(whole_in, first_row, rows_hid, 0)
    grad_b_in = lax.dynamic_slice_in_dim(whole_bias, first_row, rows_hid, 0)
    grad_w_out = lax.dynamic_slice_in_dim(whole_out, first_row, rows_hid, 0)
    return (grad_xy, grad_xz, grad_yz, grad_w_in, grad_b_in, grad_w_out)


def exchange_plan(mesh_sizes, rows_x, rows_y, levels, channels, hidden):
    chips, cores = mesh_sizes
    if levels % chips or channels % 128 or levels % cores or hidden % (chips * cores * 16):
        return None
    own_levels = levels // chips
    best = None
    for group in range(1, chips + 1):
        if chips % group or rows_y % (group * 16):
            continue
        brick_x, brick_y = rows_x * group, rows_y // group
        cost = (brick_x + brick_y) * levels
        if best is None or cost < best[0]:
            best = (cost, group, brick_x, brick_y)
    if best is None:
        return None
    _, group, brick_x, brick_y = best
    depth = None
    for tall in range(own_levels, levels // cores + 1, own_levels):
        if (levels // cores) % tall or (rows_x * tall * brick_y) % 128:
            continue
        if depth is None or brick_x * tall * brick_y <= 1024:
            depth = tall
    if depth is None or depth & (depth - 1) or brick_y & (brick_y - 1):
        return None
    return group, brick_x, brick_y, own_levels, depth


def head_kernel(
    plan, sizes, xy_in, xz_in, yz_in, lab_in, w_in, bias_in, w_out,
    gxy_out, gxz_out, gyz_out, gw_out, gb_out, go_out,
    xy_got, xz_got, yz_got, lab_got, xy_wide, xz_wide, lab_rows, w_aug, feats,
    xy_sum, xz_send, yz_send, xy_back, xz_back, yz_back,
    gw_sum, go_sum, pack, pack_got, chip_pack, chip_got, final_got,
    s_xy, r_xy, s_lab, r_lab, s_xz, r_xz, s_yz, r_yz,
    s_bxy, r_bxy, s_bxz, r_bxz, s_byz, r_byz,
    s_pk, r_pk, s_ck, r_ck, s_fin, r_fin,
):
    chips, cores = sizes
    group, brick_x, brick_y, own_levels, depth = plan
    rows_x = xy_in.shape[0]
    channels = xy_in.shape[2]
    blocks = xz_wide.shape[0]
    half_blocks = blocks // cores
    chips_per_block = depth // own_levels
    classes, hid = w_out.shape
    levels = blocks * depth
    rows = brick_x * depth * brick_y
    f32, bf16 = jnp.float32, jnp.bfloat16
    g = lax.axis_index("gx")
    c = lax.axis_index("gy")
    q = lax.rem(g, group)
    base = g - q
    me = q * cores + c

    def copy(src, dst, send, recv, chip, core):
        return pltpu.make_async_remote_copy(
            src_ref=src, dst_ref=dst, send_sem=send, recv_sem=recv,
            device_id=(chip, core), device_id_type=pl.DeviceIdType.MESH,
        )

    barrier = pltpu.get_barrier_semaphore()
    for d in range(1, chips):
        pl.semaphore_signal(barrier, inc=1, device_id=(lax.rem(g + d, chips), c), device_id_type=pl.DeviceIdType.MESH)
    for d in range(group):
        for e in range(1, cores):
            pl.semaphore_signal(
                barrier, inc=1, device_id=(base + lax.rem(q + d, group), lax.rem(c + e, cores)),
                device_id_type=pl.DeviceIdType.MESH,
            )

    def yz_copy(src_chip, to):
        rows_of = pl.ds(pl.multiple_of(lax.rem(to, group) * brick_y, brick_y), brick_y)
        return copy(yz_in.at[rows_of], yz_got.at[src_chip], s_yz.at[to], r_yz.at[src_chip], to, c)

    def xy_copy(src, to):
        rows_of = pl.ds(pl.multiple_of(to * brick_y, brick_y), brick_y)
        return copy(xy_in.at[:, rows_of], xy_got.at[src], s_xy.at[to], r_xy.at[src], base + to, c)

    def lab_copy(src, to):
        return copy(lab_in, lab_got.at[src], s_lab.at[to], r_lab.at[src], base + to, c)

    def xz_copy(src, to):
        return copy(xz_in, xz_got.at[src], s_xz.at[to], r_xz.at[src], base + to // cores, lax.rem(to, cores))

    members = group * cores
    own = pl.ds(pl.multiple_of(q * brick_y, brick_y), brick_y)
    yz_got[g] = yz_in[own, :]
    xy_got[q] = xy_in[:, own, :]
    lab_got[q] = lab_in[...]
    xz_got[me] = xz_in[...]

    bias = jnp.broadcast_to(bias_in[...], (128, hid)).T
    high = bias.astype(bf16)
    rest = bias - high.astype(f32)
    middle = rest.astype(bf16)
    low = (rest - middle.astype(f32)).astype(bf16)
    lane = lax.broadcasted_iota(jnp.int32, (hid, 128), 1)
    extra = jnp.where(
        lane == 0, high.astype(f32),
        jnp.where(lane == 1, middle.astype(f32), jnp.where(lane == 2, low.astype(f32), 0.0)),
    )
    w_aug[:, :channels] = w_in[...]
    w_aug[:, channels:] = extra.astype(bf16)
    feats[:, channels:] = jnp.ones((rows, 128), bf16)
    gw_sum[...] = jnp.zeros_like(gw_sum)
    go_sum[...] = jnp.zeros_like(go_sum)
    xy_sum[...] = jnp.zeros_like(xy_sum)

    pl.semaphore_wait(barrier, chips - 1 + group * (cores - 1))
    for d in range(1, group):
        xy_copy(q, lax.rem(q + d, group)).start()
        lab_copy(q, lax.rem(q + d, group)).start()
    for d in range(1, members):
        xz_copy(me, lax.rem(me + d, members)).start()
    for d in range(chips - 1, 0, -1):
        yz_copy(g, lax.rem(g + d, chips)).start()

    contract = lambda a, b, i, j: lax.dot_general(a, b, (((i,), (j,)), ((), ())), preferred_element_type=f32)

    y_bits, z_bits = brick_y.bit_length() - 1, depth.bit_length() - 1
    all_y = lab_in.shape[2]
    column = lax.broadcasted_iota(jnp.int32, (all_y, rows), 1)
    x_of = lax.shift_right_logical(column, y_bits + z_bits)
    same_y = lax.broadcasted_iota(jnp.int32, (all_y, rows), 0) == (column & (brick_y - 1)) + q * brick_y

    for d in range(1, group):
        xy_copy(lax.rem(q + d, group), q).wait_recv()
        lab_copy(lax.rem(q + d, group), q).wait_recv()
    xy_wide[...] = xy_got[...].astype(f32).reshape(brick_x, brick_y, channels)
    found = jnp.zeros((levels, rows), f32)
    for x in range(brick_x):
        spread = jnp.where(same_y & (x_of == x), 1.0, 0.0).astype(bf16)
        found += contract(lab_got[x // rows_x, x % rows_x].astype(f32).astype(bf16), spread, 1, 0)
    lab_rows[...] = found
    for d in range(1, members):
        xz_copy(lax.rem(me + d, members), me).wait_recv()
    for member in range(members):
        k, e = member // cores, member % cores
        for z in range(levels // cores):
            b, level = divmod(e * (levels // cores) + z, depth)
            xz_wide[b, k * rows_x:(k + 1) * rows_x, level, :] = xz_got[member, :, z * channels:(z + 1) * channels].astype(f32)


    def byz_copy(src, to):
        return copy(yz_send.at[to], yz_back.at[src], s_byz.at[to], r_byz.at[src], to, c)

    def bxz_copy(src, to, b):
        core = b // half_blocks
        j = lax.rem(b, half_blocks)
        return copy(xz_send.at[b, to], xz_back.at[src, j], s_bxz.at[b, to], r_bxz.at[src, j], base + to, core)

    def step(i, carry):
        b = lax.rem(i + g // chips_per_block, blocks)
        for k in range(chips_per_block):
            chip = b * chips_per_block + k

            @pl.when(chip != g)
            def _():
                yz_copy(chip, g).wait_recv()

        yz_block = jnp.stack([
            yz_got[b * chips_per_block + k, :, level * channels:(level + 1) * channels].astype(f32)
            for k in range(chips_per_block) for level in range(own_levels)
        ])
        total = (xy_wide[...][:, None, :, :] + xz_wide[b][:, :, None, :]) + yz_block[None]
        feats[:, :channels] = total.astype(bf16).reshape(rows, channels)
        x = contract(w_aug[...], feats[...], 1, 1)
        t = jnp.exp(-jnp.abs(x))
        u = 1.0 + t
        soft = jnp.maximum(x, 0.0) + (jnp.log(u) + (t - (u - 1.0)))
        hidden = soft.astype(bf16)
        slope = jnp.exp(x - soft)
        logits = contract(w_out[...], hidden, 1, 0)
        e = jnp.exp(logits - jnp.max(logits, axis=0, keepdims=True))
        probability = e / jnp.sum(e, axis=0, keepdims=True)
        at = lax.broadcasted_iota(jnp.int32, (levels, rows), 1)
        level_of = b * depth + (lax.shift_right_logical(at, y_bits) & (depth - 1))
        mine = lax.broadcasted_iota(jnp.int32, (levels, rows), 0) == level_of
        lab = jnp.sum(jnp.where(mine, lab_rows[...], 0.0), axis=0, keepdims=True)
        hit = lax.broadcasted_iota(jnp.int32, (classes, rows), 0).astype(f32) == lab
        dlogits = (probability - jnp.where(hit, 1.0, 0.0)).astype(bf16)
        go_sum[...] += contract(hidden, dlogits, 1, 1)
        dpre = (contract(w_out[...], dlogits, 0, 0) * slope).astype(bf16)
        gw_sum[...] += contract(dpre, feats[...], 1, 0)
        dfeat = contract(dpre, w_in[...], 0, 0).reshape(brick_x, depth, brick_y, channels)
        xy_sum[...] += jnp.sum(dfeat, axis=1)
        dyz = jnp.sum(dfeat, axis=0).reshape(chips_per_block, own_levels, brick_y, channels)
        dxz = jnp.sum(dfeat, axis=2).reshape(group, rows_x, depth, channels)
        core = b // half_blocks
        j = lax.rem(b, half_blocks)
        xz_send[b] = dxz
        for k in range(chips_per_block):
            to = b * chips_per_block + k
            yz_send[to] = dyz[k]

            @pl.when(to != g)
            def _():
                byz_copy(g, to).start()

        for k in range(group):
            @pl.when(jnp.logical_or(q != k, c != core))
            def _():
                bxz_copy(me, k, b).start()

        return carry

    lax.fori_loop(0, blocks, step, 0)

    def bxy_copy(src, to):
        rows_of = pl.ds(to * rows_x, rows_x)
        return copy(xy_sum.at[rows_of], xy_back.at[src], s_bxy.at[to], r_bxy.at[src], base + to, c)

    part_rows = hid // (chips * cores)
    pack_view = lambda a: a.reshape(chips, cores, part_rows, a.shape[-1])
    first = pack_view(gw_sum[:, :channels])
    bias_sum = gw_sum[:, channels:]
    side = jnp.where(lane == classes, bias_sum, jnp.concatenate([go_sum[...]] + [jnp.zeros((hid, 128 - classes), f32)], axis=1))
    second = pack_view(side)
    for e in range(cores):
        pack[e, :, :part_rows] = first[:, e]
        pair = second[:, e, part_rows // 2:].reshape(chips * part_rows // 2, 128)
        pack[e, :, part_rows:] = second[:, e, :part_rows // 2] + pltpu.roll(pair, 64, 1).reshape(chips, part_rows // 2, 128)

    def pk_copy(src, to):
        return copy(pack.at[to], pack_got.at[src], s_pk.at[to], r_pk.at[src], g, to)

    for d in range(1, cores):
        pk_copy(c, lax.rem(c + d, cores)).start()
    for d in range(1, group):
        bxy_copy(q, lax.rem(q + d, group)).start()
    for d in range(1, cores):
        pk_copy(lax.rem(c + d, cores), c).wait_recv()
    mine = pack[c]
    for d in range(1, cores):
        mine = mine + pack_got[lax.rem(c + d, cores)]
    chip_pack[...] = mine

    def ck_copy(src, to):
        return copy(chip_pack.at[to], chip_got.at[src], s_ck.at[to], r_ck.at[src], to, c)

    for d in range(chips - 1, 0, -1):
        ck_copy(g, lax.rem(g + d, chips)).start()

    for d in range(1, group):
        bxy_copy(lax.rem(q + d, group), q).wait_recv()
    xy_back[q] = xy_sum[pl.ds(q * rows_x, rows_x)]
    for k in range(group):
        gxy_out[:, k * brick_y:(k + 1) * brick_y, :] = xy_back[k]
    for j in range(half_blocks):
        b = c * half_blocks + j
        for d in range(1, members):
            bxz_copy(lax.rem(me + d, members), q, b).wait_recv()
        xz_back[me, j] = xz_send[b, q]
        value = xz_back[0, j]
        for k in range(1, members):
            value = value + xz_back[k, j]
        for z in range(depth):
            at = (j * depth + z) * channels
            gxz_out[:, at:at + channels] = value[:, z, :]
    for d in range(1, chips):
        byz_copy(lax.rem(g + d, chips), g).wait_recv()
    yz_back[g] = yz_send[g]
    for k in range(group):
        value = yz_back[k]
        for p in range(1, chips // group):
            value = value + yz_back[p * group + k]
        for level in range(own_levels):
            gyz_out[k * brick_y:(k + 1) * brick_y, level * channels:(level + 1) * channels] = value[level]

    for d in range(1, chips):
        ck_copy(lax.rem(g + d, chips), g).wait_recv()
    chip_got[g] = chip_pack[g]
    value = chip_got[0]
    for k in range(1, chips):
        value = value + chip_got[k]
    final_got[c] = value

    def fin_copy(src, to):
        return copy(final_got.at[src], final_got.at[src], s_fin.at[to], r_fin.at[src], g, to)

    for d in range(1, cores):
        fin_copy(c, lax.rem(c + d, cores)).start()
    for d in range(1, cores):
        fin_copy(lax.rem(c + d, cores), c).wait_recv()
    for e in range(cores):
        gw_out[e * part_rows:(e + 1) * part_rows, :] = final_got[e, :part_rows]
    halves = []
    for e in range(cores):
        both = final_got[e, part_rows:]
        halves += [both, pltpu.roll(both, 64, 1)]
    side = jnp.concatenate(halves, axis=0)
    go_out[...] = side[:, :classes]
    gb_out[...] = side.T[classes:classes + 1, :]

    for d in range(1, chips):
        to = lax.rem(g + d, chips)
        yz_copy(g, to).wait_send()
        byz_copy(g, to).wait_send()
        ck_copy(g, to).wait_send()
    for d in range(1, members):
        xz_copy(me, lax.rem(me + d, members)).wait_send()
    for d in range(1, group):
        to = lax.rem(q + d, group)
        xy_copy(q, to).wait_send()
        lab_copy(q, to).wait_send()
        bxy_copy(q, to).wait_send()
    for d in range(1, cores):
        to = lax.rem(c + d, cores)
        pk_copy(c, to).wait_send()
        fin_copy(c, to).wait_send()
    for b in range(blocks):
        for k in range(group):
            @pl.when(jnp.logical_or(q != k, c != b // half_blocks))
            def _():
                bxz_copy(me, k, b).wait_send()


def write_kernel(*refs):
    half = len(refs) // 2
    for src, dst in zip(refs[:half], refs[half:]):
        dst[...] = src[...]


def per_device_kernel(plan, sizes, plane_xy, plane_xz, plane_yz, w_in, b_in, w_out, labels):
    chips, cores = sizes
    group, brick_x, brick_y, own_levels, depth = plan
    rows_x, rows_y, channels = plane_xy.shape
    levels = labels.shape[2]
    hid, classes = w_out.shape
    blocks = levels // depth
    half_blocks = blocks // cores
    members = group * cores
    rows = brick_x * depth * brick_y
    part_rows = hid // (chips * cores)
    f32, bf16 = jnp.float32, jnp.bfloat16
    vmem = pl.BlockSpec(memory_space=pltpu.VMEM)
    dma = pltpu.SemaphoreType.DMA
    wide = channels + 128
    results = pl.pallas_call(
        functools.partial(head_kernel, plan, sizes),
        out_shape=[
            jax.ShapeDtypeStruct((rows_x, rows_y, channels), f32),
            jax.ShapeDtypeStruct(plane_xz.shape, f32),
            jax.ShapeDtypeStruct((rows_y, own_levels * channels), f32),
            jax.ShapeDtypeStruct((part_rows * cores, channels), f32),
            jax.ShapeDtypeStruct((1, part_rows * cores), f32),
            jax.ShapeDtypeStruct((part_rows * cores, classes), f32),
        ],
        in_specs=[vmem] * 7,
        out_specs=[vmem] * 6,
        scratch_shapes=[
            pltpu.VMEM((group, rows_x, brick_y, channels), bf16),
            pltpu.VMEM((members,) + plane_xz.shape, bf16),
            pltpu.VMEM((chips, brick_y, own_levels * channels), bf16),
            pltpu.VMEM((group, rows_x, levels, rows_y), jnp.int32),
            pltpu.VMEM((brick_x, brick_y, channels), f32),
            pltpu.VMEM((blocks, brick_x, depth, channels), f32),
            pltpu.VMEM((levels, rows), f32),
            pltpu.VMEM((hid, wide), bf16),
            pltpu.VMEM((rows, wide), bf16),
            pltpu.VMEM((brick_x, brick_y, channels), f32),
            pltpu.VMEM((blocks, group, rows_x, depth, channels), f32),
            pltpu.VMEM((chips, own_levels, brick_y, channels), f32),
            pltpu.VMEM((group, rows_x, brick_y, channels), f32),
            pltpu.VMEM((members, half_blocks, rows_x, depth, channels), f32),
            pltpu.VMEM((chips, own_levels, brick_y, channels), f32),
            pltpu.VMEM((hid, wide), f32),
            pltpu.VMEM((hid, classes), f32),
            pltpu.VMEM((cores, chips, 3 * part_rows // 2, 128), f32),
            pltpu.VMEM((cores, chips, 3 * part_rows // 2, 128), f32),
            pltpu.VMEM((chips, 3 * part_rows // 2, 128), f32),
            pltpu.VMEM((chips, 3 * part_rows // 2, 128), f32),
            pltpu.VMEM((cores, 3 * part_rows // 2, 128), f32),
            dma((group,)), dma((group,)), dma((group,)), dma((group,)),
            dma((members,)), dma((members,)), dma((chips,)), dma((chips,)),
            dma((group,)), dma((group,)),
            dma((blocks, group)), dma((members, half_blocks)),
            dma((chips,)), dma((chips,)),
            dma((cores,)), dma((cores,)), dma((chips,)), dma((chips,)),
            dma((cores,)), dma((cores,)),
        ],
        compiler_params=pltpu.CompilerParams(
            collective_id=0, has_side_effects=True, vmem_limit_bytes=60000 * 1024
        ),
        name="occupancy_head_backward",
    )(plane_xy, plane_xz, plane_yz, labels.transpose(0, 2, 1), w_in, b_in.reshape(1, hid), w_out.T)
    gxy, gxz, gyz, gw, gb, go = pl.pallas_call(
        write_kernel,
        out_shape=[jax.ShapeDtypeStruct(a.shape, a.dtype) for a in results],
        in_specs=[vmem] * 6,
        out_specs=[vmem] * 6,
        name="write_outputs",
    )(*results)
    return gxy, gxz, gyz, gw, gb.reshape(part_rows * cores), go


def solution(mesh):
    sizes = (mesh.shape["gx"], mesh.shape["gy"])

    def body(plane_xy, plane_xz, plane_yz, w_in, b_in, w_out, labels):
        rows_x, rows_y, channels = plane_xy.shape
        plan = exchange_plan(sizes, rows_x, rows_y, labels.shape[2], channels, w_in.shape[0])
        arrays = (plane_xy, plane_xz, plane_yz, w_in, b_in, w_out, labels)
        if plan is None or w_out.shape[1] >= 64 or plane_xy.shape[2] != 128:
            return per_device(*arrays)
        return per_device_kernel(plan, sizes, *arrays)

    placed = (P("gx", "gy", None), P("gx", "gy"), P("gy", "gx"), P(), P(), P(), P("gx", "gy", None))
    return jax.shard_map(
        body,
        mesh=mesh,
        in_specs=placed,
        out_specs=(
            P("gx", "gy", None),
            P("gx", "gy"),
            P("gy", "gx"),
            P("gx", None),
            P("gx"),
            P("gx", None),
        ),
        check_vma=False,
    )
```
